32 devices in a mesh: leaf: 4 (over x, core), front: 8 (over z, y), wave: 1.
Axes of the slice: x: 2, y: 2, z: 4, core: 2. Of those that a mesh axis runs over, the one named last changes fastest.
Arguments:
- sources: float32 [8192, 128], P(('wave', 'front')), may hold values from -48 to 48
- order: int32 [8192], P('front'), may hold values from 0 to 8191, as said below
- diagonal: float32 [8192], P(('wave', 'front')), may hold values from 0.1 to 2
- coupling: float32 [8192, 4096], P(('wave', 'front'), 'leaf'), may hold values from -0.0625 to 0.0625
- interior_inverse: float32 [64, 64, 64], P(('wave', 'leaf')), may hold values from -2 to 6, as said below
- interior_load: float32 [64, 64, 128], P(('wave', 'leaf')), may hold values from -6 to 6
Outputs:
- solution: float32 [8192, 128], P(('wave', 'front'))
- interior_solution: float32 [64, 64, 128], P(('wave', 'leaf'))
The draws below stay inside these ranges and needn't reach their ends.
Inputs may be any that keep to these rules, and one draw needn't show every extreme that they name: `order`: each aligned block of 1024 entries is a permutation of that block's own indices. `interior_inverse`: each matrix is symmetric positive definite.
All inputs are finite; a program needn't handle non-finite values.
Results may differ from the reference program's by a relative error of at most 0.0003.
Values sent between devices are 32-bit elements; how exact they have to be, the bound alone decides.
No kernel may reach another device: no remote copies, remote signals or barrier semaphores. Data moves between devices by JAX's collectives and lax.ppermute only.
A program may use at most 64 MiB of HBM per device.

```python
import math
import jax
import jax.numpy as jnp
from jax import lax

SEP_DEV = 1024
NRHS = 128
RANK = 64
ITERS = 4
SEP = 8192
BLOCKS = 64
N_FRONT = 8


def draw_sources(key, part):
    first_key, second_key = jax.random.split(key, 2)
    position = jnp.arange(SEP, dtype=jnp.float32) / SEP
    spread = jax.random.uniform(second_key, (SEP,), jnp.float32, -0.5, 0.5)
    scales = jnp.exp(jnp.log(3.0) * position + jnp.log(10.0) * spread)
    values = jnp.clip(jax.random.normal(first_key, (SEP, NRHS), jnp.float32), -5.0, 5.0)
    return values * scales[:, None]


def draw_order(key, part):
    streams = jax.random.split(key, N_FRONT)
    blocks = jax.vmap(lambda stream: jax.random.permutation(stream, SEP_DEV))(streams)
    offsets = (jnp.arange(N_FRONT, dtype=jnp.int32) * SEP_DEV)[:, None]
    return (blocks.astype(jnp.int32) + offsets).reshape(SEP)


def draw_interior_inverse(key, part):
    first_key, second_key = jax.random.split(key)
    factor = jax.random.normal(first_key, (BLOCKS, RANK, RANK), jnp.float32)
    weights = jax.random.uniform(second_key, (BLOCKS, RANK), jnp.float32, 0.5, 2.0)
    product = jnp.einsum('bij,bkj->bik', factor, factor) * (0.5 / RANK)
    return product + weights[:, :, None] * jnp.eye(RANK, dtype=jnp.float32)


def block_levels(key, dims, pieces, low, high):
    def one(dim, blocks):
        heights = jax.random.uniform(jax.random.fold_in(jax.random.fold_in(key, 6), dim), (blocks,), jnp.float32, low / len(pieces), high / len(pieces))
        return jnp.repeat(jnp.exp(heights), dims[dim] // blocks).reshape((-1,) + (1,) * (len(dims) - dim - 1))

    factor_of = one(*pieces[0])
    for cut in pieces[1:]:
        factor_of = factor_of * one(*cut)
    return factor_of


def scatter_about(key, shape, deviation, bound, cuts=(), kind=jnp.bfloat16):
    result = deviation * jax.random.normal(key, shape, jnp.float32)
    if cuts:
        result = result * block_levels(key, shape, cuts, -0.22, 0.18)
    return jnp.clip(result, -bound, bound).astype(kind)


def setup_inputs(seed: int = 0, part: int = 0) -> dict:
    key_of = jax.random.split(jax.random.key(seed), 7)
    own_keys = jax.random.split(jax.random.fold_in(key_of[6], part), 7)
    sources = draw_sources(jax.random.fold_in(jax.random.fold_in(key_of[6], part), 71), part)
    order = draw_order(jax.random.fold_in(key_of[6], 71), part)
    diagonal = jnp.clip(jnp.exp(math.log(2.0) - 2.9957323 * jax.random.uniform(own_keys[2], (SEP,), jnp.float32) ** block_levels(own_keys[2], (SEP,), ((0, 8),), -0.2, 0.2)), 0.1, 2.0)
    coupling = scatter_about(own_keys[3], (SEP, BLOCKS * RANK), (2 * RANK * BLOCKS) ** -0.5, 0.0625, ((0, 8), (1, 4)), jnp.float32)
    interior_inverse = draw_interior_inverse(jax.random.fold_in(jax.random.fold_in(key_of[6], part), 71), part)
    interior_load = scatter_about(own_keys[5], (BLOCKS, RANK, NRHS), 1.0, 6.0, ((0, 4),), jnp.float32)
    return dict(sources=sources, order=order, diagonal=diagonal, coupling=coupling, interior_inverse=interior_inverse, interior_load=interior_load)


HIGHEST = lax.Precision.HIGHEST


def reference(sources, order, diagonal, coupling, interior_inverse, interior_load):
    loads = jnp.take(sources, order.astype(jnp.int32), axis=0)

    def condense(projected):
        shaped = projected.reshape(BLOCKS, RANK, NRHS)
        return jnp.einsum("bij,bjn->bin", interior_inverse, shaped, precision=HIGHEST)

    def operate(direction):
        projected = jnp.einsum("sk,sn->kn", coupling, direction, precision=HIGHEST)
        coeffs = condense(projected).reshape(BLOCKS * RANK, NRHS)
        return diagonal[:, None] * direction + jnp.einsum("sk,kn->sn", coupling, coeffs, precision=HIGHEST)

    solution = jnp.zeros_like(loads)
    residual = loads
    direction = loads
    norm_now = jnp.sum(residual * residual, axis=0)
    for iteration in range(ITERS):
        image = operate(direction)
        step_size = norm_now / jnp.sum(direction * image, axis=0)
        solution = solution + step_size * direction
        residual = residual - step_size * image
        norm_next = jnp.sum(residual * residual, axis=0)
        direction = residual + (norm_next / norm_now) * direction
        norm_now = norm_next
    projected = jnp.einsum("sk,sn->kn", coupling, solution, precision=HIGHEST).reshape(BLOCKS, RANK, NRHS)
    interior_solution = jnp.einsum("bij,bjn->bin", interior_inverse, interior_load - projected, precision=HIGHEST)
    return (solution, interior_solution)
```

```python
import jax
import jax.numpy as jnp
from jax import lax
from jax.sharding import PartitionSpec as P

ITERS = 4
PASSES = lax.Precision.HIGH
BOTH = ("leaf", "front")


def pairs_of(n_leaf, n_front, partner):
    found = []
    for leaf in range(n_leaf):
        for front in range(n_front):
            to_leaf, to_front = partner(leaf, front)
            found.append((leaf * n_front + front, to_leaf * n_front + to_front))
    return found


def pick(halves, bit):
    return lax.dynamic_index_in_dim(halves, bit, 0, keepdims=False)


def joined(own, other, bit):
    first = jnp.where(bit == 0, own, other)
    second = jnp.where(bit == 0, other, own)
    return jnp.concatenate([first, second], axis=0)


class Exchange:
    def __init__(self, n_leaf, n_front):
        self.sizes = (n_leaf, n_front)
        assert n_leaf & (n_leaf - 1) == 0 and n_front & (n_front - 1) == 0
        assert n_leaf >= 2 and n_front >= 4
        leaf, front = lax.axis_index("leaf"), lax.axis_index("front")
        odd = leaf % 2
        low, high = front % 2, (front // 2) % 2
        self.first_bit = jnp.where(odd == 0, low, high)
        self.second_bit = jnp.where(odd == 0, high, low)
        self.core_bit = odd

    def swap(self, value, partner):
        return lax.ppermute(value, BOTH, pairs_of(*self.sizes, partner))

    def first(self, leaf, front):
        return leaf, front ^ (1 if leaf % 2 == 0 else 2)

    def second(self, leaf, front):
        return leaf, front ^ (2 if leaf % 2 == 0 else 1)

    def over_front(self, value, extra):
        columns = value.shape[1]

        def scatter(value, extra, partner, bit):
            halves = value.reshape(2, -1, columns)
            message = jnp.concatenate([pick(halves, 1 - bit), extra], axis=0)
            came = self.swap(message, partner)
            rows = halves.shape[1]
            return pick(halves, bit) + came[:rows], extra + came[rows:]

        half, extra = scatter(value, extra, self.first, self.first_bit)
        quarter, extra = scatter(half, extra, self.second, self.second_bit)
        message = jnp.concatenate([quarter, extra], axis=0)
        distance = 4
        while distance < self.sizes[1]:
            message = message + self.swap(message, lambda l, f, d=distance: (l, f ^ d))
            distance *= 2
        rows = quarter.shape[0]
        quarter, extra = message[:rows], message[rows:]
        half = joined(quarter, self.swap(quarter, self.second), self.second_bit)
        return joined(half, self.swap(half, self.first), self.first_bit), extra

    def over_leaf(self, value, extra):
        columns = value.shape[1]
        halves = value.reshape(2, -1, columns)
        rows = halves.shape[1]
        core = lambda l, f: (l ^ 1, f)
        came = self.swap(
            jnp.concatenate([pick(halves, 1 - self.core_bit), extra], axis=0), core
        )
        message = jnp.concatenate([pick(halves, self.core_bit), extra], axis=0) + came
        message = self.chips(message)
        half, extra = message[:rows], message[rows:]
        return joined(half, self.swap(half, core), self.core_bit), extra

    def chips(self, message):
        distance = 2
        while distance < self.sizes[0]:
            message = message + self.swap(message, lambda l, f, d=distance: (l ^ d, f))
            distance *= 2
        return message

    def small_over_leaf(self, extra):
        extra = extra + self.swap(extra, lambda l, f: (l ^ 1, f))
        return self.chips(extra)


def rows_of(*rows):
    filled = list(rows) + [jnp.zeros_like(rows[0])] * (8 - len(rows))
    return jnp.stack(filled)


def solver(n_leaf, n_front):
    def per_device(sources, order, diagonal, coupling, interior_inverse, interior_load):
        net = Exchange(n_leaf, n_front)
        columns = sources.shape[1]
        rank = interior_inverse.shape[1]
        positions = order - lax.axis_index("front") * sources.shape[0]
        loads = jnp.take(sources, positions, axis=0)
        scale = diagonal[:, None]

        def condense(projected):
            shaped = projected.reshape(-1, rank, columns)
            return jnp.einsum("bij,bjn->bin", interior_inverse, shaped, precision=PASSES)

        residual = loads
        direction = projected = solution = gathered = None
        norm = weighted = None
        for iteration in range(ITERS):
            partial = jnp.einsum("sk,sn->kn", coupling, residual, precision=PASSES)
            scaled = scale * residual
            sums = [jnp.sum(residual * residual, axis=0), jnp.sum(scaled * residual, axis=0)]
            if iteration > 0:
                sums.append(jnp.sum(scaled * direction, axis=0))
            total, extra = net.over_front(partial, rows_of(*sums))
            if iteration == 0:
                norm, weighted = extra[0], extra[1]
                projected, direction = total, residual
            else:
                ratio = extra[0] / norm
                weighted = extra[1] + 2.0 * ratio * extra[2] + ratio * ratio * weighted
                norm = extra[0]
                projected = total + ratio * projected
                direction = residual + ratio * direction
            coeffs = condense(projected).reshape(-1, columns)
            energy = rows_of(jnp.sum(projected * coeffs, axis=0))
            if iteration < ITERS - 1:
                spread = jnp.einsum("sk,kn->sn", coupling, coeffs, precision=PASSES)
                spread, energy = net.over_leaf(spread, energy)
            else:
                energy = net.small_over_leaf(energy)
            step = norm / (weighted + energy[0])
            if iteration == 0:
                solution, gathered = step * direction, step * projected
            else:
                solution, gathered = solution + step * direction, gathered + step * projected
            if iteration < ITERS - 1:
                residual = residual - step * (scale * direction + spread)
        missing = interior_load - gathered.reshape(interior_load.shape)
        return solution, condense(missing)

    return per_device


def solution(mesh):
    return jax.shard_map(
        solver(mesh.shape["leaf"], mesh.shape["front"]),
        mesh=mesh,
        in_specs=(
            P(("wave", "front"), None),
            P("front"),
            P(("wave", "front")),
            P(("wave", "front"), "leaf"),
            P(("wave", "leaf"), None, None),
            P(("wave", "leaf"), None, None),
        ),
        out_specs=(P(("wave", "front"), None), P(("wave", "leaf"), None, None)),
        check_vma=False,
    )
```

```python
import functools

import jax
import jax.numpy as jnp
from jax import lax
from jax.experimental import pallas as pl
from jax.experimental.pallas import tpu as pltpu
from jax.sharding import PartitionSpec as P

ITERS = 4
EXTRA = 8
F32, BF16 = jnp.float32, jnp.bfloat16
AXES = ("leaf", "front", "wave")


def halves_of(value):
    high = value.astype(BF16)
    return high, (value - high.astype(F32)).astype(BF16)


def product(left_high, left_low, right):
    columns = right.shape[1] // 2
    whole = jnp.dot(left_high, right, preferred_element_type=F32)
    rest = jnp.dot(left_low, right[:, :columns], preferred_element_type=F32)
    return whole[:, :columns] + whole[:, columns:] + rest


def side_by_side(value):
    return jnp.concatenate(halves_of(value), axis=1)


def call(kernel, outs, scalars, *operands, scratch=(), name=None):
    vmem = pl.BlockSpec(memory_space=pltpu.VMEM)
    return pl.pallas_call(
        kernel,
        name=name,
        out_shape=[jax.ShapeDtypeStruct(shape, dtype) for shape, dtype in outs],
        in_specs=[pl.BlockSpec(memory_space=pltpu.SMEM)] + [vmem] * len(operands),
        out_specs=[vmem] * len(outs),
        scratch_shapes=list(scratch),
        compiler_params=pltpu.CompilerParams(vmem_limit_bytes=20 << 20),
    )(scalars, *operands)


def gather_kernel(place_ref, sources_ref, loads_ref):
    rows = loads_ref.shape[0]
    group = 8

    def body(step, _):
        for i in range(group):
            at = step * group + i
            loads_ref[pl.ds(at, 1), :] = sources_ref[pl.ds(place_ref[at], 1), :]
        return 0

    lax.fori_loop(0, rows // group, body, 0)


def blocks_kernel(_, inverse_ref, high_ref, low_ref):
    groups, width, _ = high_ref.shape
    rank = inverse_ref.shape[1]
    each = width // rank
    high_ref[...] = jnp.zeros_like(high_ref)
    low_ref[...] = jnp.zeros_like(low_ref)
    for group in range(groups):
        for i in range(each):
            at = pl.ds(i * rank, rank)
            high_ref[group, at, at], low_ref[group, at, at] = halves_of(inverse_ref[group * each + i])


def write_messages(place_ref, residual, scaled, direction_scaled, forward_high, forward_low, out_ref):
    me = place_ref[0]
    sums = [jnp.sum(residual * residual, axis=0, keepdims=True), jnp.sum(scaled * residual, axis=0, keepdims=True)]
    if direction_scaled is not None:
        sums.append(jnp.sum(residual * direction_scaled, axis=0, keepdims=True))
    sums.append(jnp.zeros((EXTRA - len(sums), residual.shape[1]), F32))
    sums = jnp.concatenate(sums, axis=0)
    right = side_by_side(residual)
    quarter = forward_high.shape[0] // 4
    for q in range(4):
        rows = pl.ds(q * quarter, quarter)
        out_ref[q ^ me, :quarter, :] = product(forward_high[rows, :], forward_low[rows, :], right)
        out_ref[q ^ me, quarter:, :] = sums


def first_kernel(place_ref, residual_ref, scale_ref, forward_high, forward_low, out_ref):
    residual = residual_ref[...]
    write_messages(place_ref, residual, scale_ref[...] * residual, None, forward_high, forward_low, out_ref)


def update_kernel(
    place_ref, state_ref, own_ref, other_ref, residual_ref, direction_scaled_ref, scale_ref, forward_high, forward_low,
    next_ref, step_ref, out_ref,
):
    core = place_ref[1]
    half = other_ref.shape[0]
    step = state_ref[1:2, :] / (state_ref[2:3, :] + own_ref[half:half + 1, :])
    step_ref[...] = jnp.broadcast_to(step, step_ref.shape)
    for part, ref in ((core, own_ref), (1 - core, other_ref)):
        rows = pl.ds(pl.multiple_of(part * half, half), half)
        next_ref[rows, :] = residual_ref[rows, :] - step * (direction_scaled_ref[rows, :] + ref[:half, :])
    residual = next_ref[...]
    write_messages(
        place_ref, residual, scale_ref[...] * residual, direction_scaled_ref[...], forward_high, forward_low, out_ref
    )


def condense_kernel(first, place_ref, here_ref, came_ref, *refs):
    if first:
        high_ref, low_ref, projected_ref, state_ref, out_ref = refs
    else:
        before_ref, last_ref, high_ref, low_ref, projected_ref, state_ref, out_ref = refs
    me = place_ref[0]
    rows = projected_ref.shape[0]
    total = here_ref[...] + came_ref[...]
    norm, weighted = total[rows:rows + 1], total[rows + 1:rows + 2]
    projected = total[:rows]
    ratio = jnp.zeros_like(norm)
    if not first:
        ratio = norm / last_ref[1:2, :]
        weighted = weighted + 2.0 * ratio * total[rows + 2:rows + 3] + ratio * ratio * last_ref[2:3, :]
        projected = projected + ratio * before_ref[...]
    projected_ref[...] = projected
    state_ref[...] = jnp.concatenate([ratio, norm, weighted, jnp.zeros((EXTRA - 3, norm.shape[1]), F32)], axis=0)
    coeffs = product(high_ref[me], low_ref[me], side_by_side(projected))
    out_ref[:rows, :] = coeffs
    out_ref[rows:, :] = jnp.broadcast_to(jnp.sum(projected * coeffs, axis=0, keepdims=True), (EXTRA, norm.shape[1]))


def direction_kernel(
    place_ref, state_ref, residual_ref, direction_ref, scale_ref, out_ref, scaled_ref
):
    direction = residual_ref[...] + state_ref[0:1, :] * direction_ref[...]
    out_ref[...] = direction
    scaled_ref[...] = scale_ref[...] * direction


def gain_kernel(first, place_ref, step_ref, direction_ref, c0, c1, c2, c3, *refs):
    if first:
        solution_ref, gathered_ref = refs
    else:
        solution_in, gathered_in, solution_ref, gathered_ref = refs
    step = step_ref[0:1, :]
    rows = gathered_ref.shape[1]
    gain = step * direction_ref[...]
    solution_ref[...] = gain if first else solution_in[...] + gain
    for slot, ref in enumerate((c0, c1, c2, c3)):
        gain = step * ref[:rows, :]
        gathered_ref[slot] = gain if first else gathered_in[slot] + gain


def spread_kernel(place_ref, c0, c1, c2, c3, back_high, back_low, out_ref, right_ref):
    me, core = place_ref[0], place_ref[1]
    quarter = right_ref.shape[0] // 4
    columns = out_ref.shape[2]
    energy = jnp.zeros((EXTRA, columns), F32)
    for slot, ref in enumerate((c0, c1, c2, c3)):
        rows = pl.ds(pl.multiple_of((me ^ slot) * quarter, quarter), quarter)
        right_ref[rows, :] = side_by_side(ref[:quarter, :])
        energy = energy + ref[quarter:, :]
    right = right_ref[...]
    half = back_high.shape[0] // 2
    for part in range(2):
        rows = pl.ds(part * half, half)
        out_ref[part ^ core, :half, :] = product(back_high[rows, :], back_low[rows, :], right)
        out_ref[part ^ core, half:, :] = energy


def finish_kernel(
    place_ref, state_ref, energy_ref, direction_ref, c0, c1, c2, c3, solution_in, gathered_in, interior_ref,
    solution_ref, out_ref,
):
    me = place_ref[0]
    step = state_ref[1:2, :] / (state_ref[2:3, :] + energy_ref[0:1, :])
    solution_ref[...] = solution_in[...] + step * direction_ref[...]
    quarter = gathered_in.shape[1]
    for slot, ref in enumerate((c0, c1, c2, c3)):
        rows = pl.ds(pl.multiple_of((me ^ slot) * quarter, quarter), quarter)
        out_ref[rows, :] = interior_ref[rows, :] - (gathered_in[slot] + step * ref[:quarter, :])


def interior_kernel(_, load_ref, high_ref, low_ref, out_ref):
    groups, width, _ = high_ref.shape
    for group in range(groups):
        rows = pl.ds(group * width, width)
        out_ref[rows, :] = product(high_ref[group], low_ref[group], side_by_side(load_ref[rows, :]))


def solver(n_leaf, n_front):
    assert n_leaf & (n_leaf - 1) == 0 and n_front & (n_front - 1) == 0
    assert n_leaf >= 2 and n_front >= 4

    def swap(value, leaf_mask, front_mask):
        pairs = [
            (leaf * n_front + front, (leaf ^ leaf_mask) * n_front + (front ^ front_mask))
            for leaf in range(n_leaf)
            for front in range(n_front)
        ]
        return lax.ppermute(value, AXES, pairs)

    def all_over(value, size, start, axis):
        mask = start
        while mask < size:
            value = value + (swap(value, mask, 0) if axis == 0 else swap(value, 0, mask))
            mask *= 2
        return value

    def per_device(sources, order, diagonal, coupling, interior_inverse, interior_load):
        rows, columns = sources.shape
        width = coupling.shape[1]
        quarter, half = width // 4, rows // 2
        blocks, rank, _ = interior_inverse.shape
        leaf, front = lax.axis_index("leaf"), lax.axis_index("front")
        place = jnp.stack([front % 4, leaf % 2]).astype(jnp.int32)
        message = ((quarter + EXTRA, columns), F32)
        field = ((rows, columns), F32)
        small = ((EXTRA, columns), F32)

        def split(value):
            high = lax.reduce_precision(value, 8, 7)
            return high.astype(BF16), (value - high).astype(BF16)

        back = split(coupling)
        forward = tuple(piece.T for piece in back)
        (loads,) = call(gather_kernel, [field], order - front * rows, sources, name="gather")
        scale = jnp.broadcast_to(diagonal[:, None], (rows, columns))
        inverse = call(
            blocks_kernel, [((4, quarter, quarter), BF16)] * 2, place, interior_inverse, name="blocks"
        )
        (interior,) = call(
            interior_kernel, [((blocks * rank, columns), F32)], place, interior_load.reshape(-1, columns), *inverse,
            name="interior",
        )

        def over_front(messages):
            came = [swap(messages[slot], 0, slot) for slot in (3, 1, 2)]
            here = messages[0] + came[0] + came[1] + came[2]
            mask = 4
            while mask * 2 < n_front:
                here = here + swap(here, 0, mask)
                mask *= 2
            return here, (swap(here, 0, mask) if mask < n_front else jnp.zeros_like(here))

        residual = direction = loads
        direction_scaled = projected = state = solution = gathered = step = coeffs = None
        (messages,) = call(
            first_kernel, [((4, quarter + EXTRA, columns), F32)], place, loads, scale, *forward, name="project"
        )
        for iteration in range(ITERS):
            here, came = over_front(messages)
            before = () if iteration == 0 else (projected, state)
            projected, state, own = call(
                functools.partial(condense_kernel, iteration == 0),
                [((quarter, columns), F32), small, message],
                place, here, came, *before, *inverse, name="condense",
            )
            others = {slot: swap(own, 0, slot) for slot in (3, 1, 2)}
            if iteration > 0:
                held = () if iteration == 1 else (solution, gathered)
                solution, gathered = call(
                    functools.partial(gain_kernel, iteration == 1),
                    [field, ((4, quarter, columns), F32)],
                    place, step, direction, *coeffs, *held, name="gain",
                )
                direction, direction_scaled = call(
                    direction_kernel, [field, field], place, state, residual, direction, scale, name="direction"
                )
            else:
                direction_scaled = scale * direction
            coeffs = [own, others[1], others[2], others[3]]
            if iteration == ITERS - 1:
                energy = sum(piece[quarter:] for piece in coeffs)
                energy = all_over(energy, n_leaf, 1, 0)
                solution, interior = call(
                    finish_kernel, [field, ((blocks * rank, columns), F32)],
                    place, state, energy, direction, *coeffs, solution, gathered, interior, name="finish",
                )
                break
            (spread,) = call(
                spread_kernel, [((2, half + EXTRA, columns), F32)], place, *coeffs, *back,
                scratch=[pltpu.VMEM((width, 2 * columns), BF16)], name="spread",
            )
            mine = all_over(spread[0] + swap(spread[1], 1, 0), n_leaf, 2, 0)
            other = swap(mine[:half], 1, 0)
            residual, step, messages = call(
                update_kernel, [field, small, ((4, quarter + EXTRA, columns), F32)],
                place, state, mine, other, residual, direction_scaled, scale, *forward, name="update",
            )
        return solution, interior.reshape(interior_load.shape)

    return per_device


def solution(mesh):
    return jax.shard_map(
        solver(mesh.shape["leaf"], mesh.shape["front"]),
        mesh=mesh,
        in_specs=(
            P(("wave", "front"), None),
            P("front"),
            P(("wave", "front")),
            P(("wave", "front"), "leaf"),
            P(("wave", "leaf"), None, None),
            P(("wave", "leaf"), None, None),
        ),
        out_specs=(P(("wave", "front"), None), P(("wave", "leaf"), None, None)),
        check_vma=False,
    )
```

```python
import functools
import math

import jax
import jax.numpy as jnp
from jax import lax
from jax.experimental import pallas as pl
from jax.experimental.pallas import tpu as pltpu
from jax.sharding import PartitionSpec as P


ITERS = 4
GROUPS = 2
EXTRA = 8
LANES = 128
GRANT = 24 << 20
F32, BF16 = jnp.float32, jnp.bfloat16
AXES = ("leaf", "front", "wave")


def halves_of(value):
    high = value.astype(BF16)
    return high, (value - high.astype(F32)).astype(BF16)


def stacked(value):
    return jnp.concatenate(halves_of(value), axis=0)


def product(left, high, low):
    rows = left.shape[0] // 2
    whole = jnp.dot(left, high, preferred_element_type=F32)
    return whole[:rows] + whole[rows:] + jnp.dot(left[:rows], low, preferred_element_type=F32)


def as_rows(columns, width):
    sources = columns[0].shape[0]
    lane = lax.broadcasted_iota(jnp.int32, (sources, LANES), 1)
    table = jnp.zeros((sources, LANES), F32)
    for at, column in enumerate(columns):
        table = jnp.where(lane == at, column, table)
    turned = table.T[:EXTRA, :]
    return jnp.concatenate([turned, jnp.zeros((EXTRA, width - sources), F32)], axis=1)


def as_columns(rows, sources):
    block = jnp.concatenate([rows[:, :LANES], jnp.zeros((LANES - EXTRA, LANES), F32)], axis=0)
    return block.T[:sources, :]


def total_of(value):
    return jnp.sum(value, axis=1, keepdims=True)


def quarter_here():
    return lax.rem(lax.axis_index("front"), 4)


def core_here():
    return lax.rem(lax.axis_index("leaf"), 2)


def call(kernel, outs, *operands, scratch=(), flops=0, apart=(), grant=24 << 20):
    vmem = pl.BlockSpec(memory_space=pltpu.VMEM)
    anywhere = pl.BlockSpec(memory_space=pltpu.HBM)
    moved = sum(math.prod(shape) * jnp.dtype(dtype).itemsize for shape, dtype in outs)
    moved += sum(operand.size * operand.dtype.itemsize for operand in operands + tuple(apart))
    return pl.pallas_call(
        kernel,
        out_shape=[jax.ShapeDtypeStruct(shape, dtype) for shape, dtype in outs],
        in_specs=[anywhere] * len(apart) + [vmem] * len(operands),
        out_specs=[vmem] * len(outs),
        scratch_shapes=list(scratch),
        cost_estimate=pl.CostEstimate(flops=flops, bytes_accessed=moved, transcendentals=0),
        compiler_params=pltpu.CompilerParams(vmem_limit_bytes=grant),
    )(*apart, *operands)


def blocks_kernel(inverse_ref, high_ref, low_ref):
    count, width, _ = high_ref.shape
    rank = inverse_ref.shape[1]
    each = width // rank
    high_ref[...] = jnp.zeros_like(high_ref)
    low_ref[...] = jnp.zeros_like(low_ref)
    for at in range(count):
        for i in range(each):
            own = pl.ds(i * rank, rank)
            high_ref[at, own, own], low_ref[at, own, own] = halves_of(inverse_ref[at * each + i].T)


def interior_kernel(load_ref, high_ref, low_ref, out_ref):
    count, width, _ = high_ref.shape
    for at in range(count):
        own = pl.ds(at * width, width)
        out_ref[:, own] = product(stacked(load_ref[own, :].T), high_ref[at], low_ref[at])


def turn_kernel(coupling_ref, high_ref, low_ref):
    rows = high_ref.shape[0]
    for part in range(8):
        own = pl.ds(part * (rows // 8), rows // 8)
        high_ref[own, :], low_ref[own, :] = halves_of(coupling_ref[:, own].T)


def write_messages(me, residual, scaled, direction_scaled, high_ref, low_ref, out_ref):
    sources, quarter = residual.shape[0], out_ref.shape[2]
    sums = [total_of(residual * residual), total_of(scaled * residual)]
    if direction_scaled is not None:
        sums.append(total_of(residual * direction_scaled))
    sums = as_rows(sums, quarter)
    left = stacked(residual)
    for q in range(4):
        own = pl.ds(q * quarter, quarter)
        out_ref[q ^ me, :sources, :] = product(left, high_ref[:, own], low_ref[:, own])
        out_ref[q ^ me, sources:, :] = sums


def start_kernel(
    sources_hbm, coupling_hbm, order_hbm, diagonal_hbm,
    loads_a_ref, loads_b_ref, high_ref, low_ref, scale_ref, out_ref,
    sources_ref, coupling_ref, gathered_ref, order_ref, sems, small_sems,
):
    listed = pltpu.make_async_copy(order_hbm, order_ref, small_sems.at[0])
    scaled = pltpu.make_async_copy(diagonal_hbm, scale_ref, small_sems.at[1])
    taken = pltpu.make_async_copy(sources_hbm, sources_ref, sems.at[0])
    rows, parts = high_ref.shape[0], coupling_ref.shape[0]
    each = rows // parts
    copies = [
        pltpu.make_async_copy(coupling_hbm.at[pl.ds(i * each, each), :], coupling_ref.at[i], sems.at[1 + i])
        for i in range(parts)
    ]
    listed.start()
    taken.start()
    scaled.start()
    for copy in copies:
        copy.start()
    listed.wait()
    taken.wait()
    base = lax.axis_index("front") * high_ref.shape[0]
    group = 16

    def body(step, _):
        for i in range(group):
            at = step * group + i
            gathered_ref[pl.ds(at, 1), :] = sources_ref[pl.ds(order_ref[at] - base, 1), :]
        return 0

    lax.fori_loop(0, rows // group, body, 0)
    loads = gathered_ref[...].T
    half = loads.shape[0] // 2
    loads_a_ref[...], loads_b_ref[...] = loads[:half], loads[half:]
    for i, copy in enumerate(copies):
        copy.wait()
        own = pl.ds(i * each, each)
        high_ref[own, :], low_ref[own, :] = halves_of(coupling_ref[i])
    first = loads[:half]
    scaled.wait()
    write_messages(quarter_here(), first, scale_ref[...] * first, None, high_ref, low_ref, out_ref)


def first_kernel(loads_ref, diagonal_ref, high_ref, low_ref, out_ref):
    loads = loads_ref[...]
    write_messages(quarter_here(), loads, diagonal_ref[...] * loads, None, high_ref, low_ref, out_ref)


def update_kernel(
    state_ref, own_ref, other_ref, residual_ref, direction_ref, diagonal_ref, high_ref, low_ref,
    next_ref, step_ref, out_ref,
):
    me, core = quarter_here(), core_here()
    sources, half = other_ref.shape
    energy = as_columns(own_ref[sources:, :], sources)[:, 0:1]
    step = state_ref[1, :, 0:1] / (state_ref[2, :, 0:1] + energy)
    step_ref[...] = jnp.broadcast_to(step, step_ref.shape)
    for part, ref in ((core, own_ref), (1 - core, other_ref)):
        own = pl.ds(pl.multiple_of(part * half, half), half)
        image = diagonal_ref[:, own] * direction_ref[:, own] + ref[:sources, :]
        next_ref[:, own] = residual_ref[:, own] - step * image
    residual = next_ref[...]
    diagonal = diagonal_ref[...]
    write_messages(me, residual, diagonal * residual, diagonal * direction_ref[...], high_ref, low_ref, out_ref)


def condense_kernel(first, joint, here_ref, came_ref, *refs):
    refs = list(refs)
    before_ref, last_ref = (None, None) if first else (refs.pop(0), refs.pop(0))
    held_ref = refs.pop(0) if joint else None
    high_ref, low_ref, projected_ref, state_ref, out_ref = refs
    me = quarter_here()
    sources, quarter = projected_ref.shape
    total = here_ref[...] + came_ref[...]
    sums = as_columns(total[sources:], sources)
    norm, weighted = sums[:, 0:1], sums[:, 1:2]
    projected = total[:sources]
    ratio = jnp.zeros_like(norm)
    if not first:
        ratio = norm / last_ref[1, :, 0:1]
        weighted = weighted + 2.0 * ratio * sums[:, 2:3] + ratio * ratio * last_ref[2, :, 0:1]
        projected = projected + ratio * before_ref[...]
    projected_ref[...] = projected
    for at, value in enumerate((ratio, norm, weighted)):
        state_ref[at] = jnp.broadcast_to(value, (sources, LANES))
    coeffs = product(stacked(projected), high_ref[me], low_ref[me])
    out_ref[:sources, :] = coeffs
    energy = as_rows([total_of(projected * coeffs)], quarter)
    if held_ref is not None:
        row = lax.broadcasted_iota(jnp.int32, energy.shape, 0)
        energy = jnp.where(row == 1, energy[0:1, :], held_ref[sources:, :])
    out_ref[sources:, :] = energy


def advance_kernel(first, state_ref, step_ref, residual_ref, direction_ref, *refs):
    refs = list(refs)
    pieces, refs = refs[:4], refs[4:]
    solution_in, gathered_in = (None, None) if first else (refs.pop(0), refs.pop(0))
    next_ref, solution_ref, gathered_ref = refs
    step = step_ref[:, 0:1]
    direction = direction_ref[...]
    gain = step * direction
    solution_ref[...] = gain if first else solution_in[...] + gain
    sources = direction.shape[0]
    for slot, ref in enumerate(pieces):
        gain = step * ref[:sources, :]
        gathered_ref[slot] = gain if first else gathered_in[slot] + gain
    next_ref[...] = residual_ref[...] + state_ref[0, :, 0:1] * direction


def spread_kernel(c0, c1, c2, c3, high_ref, low_ref, out_ref, left_ref):
    me, core = quarter_here(), core_here()
    sources, quarter = c0.shape[0] - EXTRA, c0.shape[1]
    pieces = (c0, c1, c2, c3)
    for slot, ref in enumerate(pieces):
        own = pl.ds(pl.multiple_of((me ^ slot) * quarter, quarter), quarter)
        left_ref[:, own] = stacked(ref[:sources, :])
    energy = c0[sources:, :] + c1[sources:, :] + c2[sources:, :] + c3[sources:, :]
    left = left_ref[...]
    half = high_ref.shape[1] // 2
    chunk = min(half, 256)
    for part in range(2):
        for at in range(0, half, chunk):
            own = pl.ds(part * half + at, chunk)
            out_ref[part ^ core, :sources, pl.ds(at, chunk)] = product(left, high_ref[:, own], low_ref[:, own])
        out_ref[part ^ core, sources:, :] = jnp.concatenate(
            [energy[:, :LANES], jnp.zeros((EXTRA, half - LANES), F32)], axis=1
        )


def finish_kernel(interior_ref, energy_ref, *refs):
    inputs, (solution_ref, out_ref, left_ref) = refs[:-3], refs[-3:]
    me = quarter_here()
    each = len(inputs) // GROUPS
    energies = as_columns(energy_ref[...], left_ref.shape[0] // GROUPS)
    found = []
    for group in range(GROUPS):
        state_ref, direction_ref, *pieces, solution_in, gathered_in = inputs[group * each:(group + 1) * each]
        sources, quarter = pieces[0].shape[0] - EXTRA, pieces[0].shape[1]
        energy = energies[:, group:group + 1]
        step = state_ref[1, :, 0:1] / (state_ref[2, :, 0:1] + energy)
        found.append(solution_in[...] + step * direction_ref[...])
        rows = pl.ds(group * sources, sources)
        for slot, ref in enumerate(pieces):
            own = pl.ds(pl.multiple_of((me ^ slot) * quarter, quarter), quarter)
            left_ref[rows, own] = interior_ref[rows, own] - (gathered_in[slot] + step * ref[:sources, :])
    solution_ref[...] = jnp.concatenate(found, axis=0).T
    out_ref[...] = left_ref[...].T


def solver(n_leaf, n_front):
    assert n_leaf & (n_leaf - 1) == 0 and n_front & (n_front - 1) == 0
    assert n_leaf >= 2 and n_front >= 4

    def swap(value, leaf_mask, front_mask):
        pairs = [
            (leaf * n_front + front, (leaf ^ leaf_mask) * n_front + (front ^ front_mask))
            for leaf in range(n_leaf)
            for front in range(n_front)
        ]
        return lax.ppermute(value, AXES, pairs)

    def over_leaf(value):
        mask = 2
        while mask < n_leaf:
            value = value + swap(value, mask, 0)
            mask *= 2
        return value

    def over_near(messages):
        here = messages[0]
        for slot in (3, 1, 2):
            here = here + swap(messages[slot], 0, slot)
        return here

    def over_far(here):
        mask = 4
        while mask * 2 < n_front:
            here = here + swap(here, 0, mask)
            mask *= 2
        return here, (swap(here, 0, mask) if mask < n_front else jnp.zeros_like(here))

    def gathered_from(own):
        others = {}
        for slot in (3, 1, 2):
            others[slot] = swap(own, 0, slot)
        return [own, others[1], others[2], others[3]]

    def per_device(sources, order, diagonal, coupling, interior_inverse, interior_load):
        rows, columns = sources.shape
        width = coupling.shape[1]
        quarter, half, each = width // 4, rows // 2, columns // GROUPS
        blocks, rank, _ = interior_inverse.shape
        field = ((each, rows), F32)
        message = ((each + EXTRA, quarter), F32)
        messages_of = ((4, each + EXTRA, quarter), F32)
        state_of = ((3, each, LANES), F32)
        work = 6 * rows * width * each

        parts = 8
        *loads, high, low, scale, messages = call(
            start_kernel, [field, field] + [((rows, width), BF16)] * 2 + [((1, rows), F32), messages_of],
            apart=(sources, coupling, order, diagonal.reshape(1, rows)), flops=work, grant=GRANT,
            scratch=[
                pltpu.VMEM((rows, columns), F32), pltpu.VMEM((parts, rows // parts, width), F32),
                pltpu.VMEM((rows, columns), F32), pltpu.SMEM((rows,), jnp.int32),
                pltpu.SemaphoreType.DMA((1 + parts,)), pltpu.SemaphoreType.DMA((2,)),
            ],
        )
        here = [over_near(messages)]
        (messages,) = call(first_kernel, [messages_of], loads[1], scale, high, low, flops=work)
        here.append(over_near(messages))
        back = call(turn_kernel, [((width, rows), BF16)] * 2, coupling)
        inverse = call(blocks_kernel, [((4, quarter, quarter), BF16)] * 2, interior_inverse)
        (interior,) = call(
            interior_kernel, [((columns, blocks * rank), F32)], interior_load.reshape(-1, columns), *inverse,
        )

        class Group:
            pass

        groups = []
        for n in range(GROUPS):
            g = Group()
            g.residual = g.direction = loads[n]
            g.here = here[n]
            g.step = g.state = g.projected = g.solution = g.gathered = g.coeffs = None
            groups.append(g)

        def iterate(g, iteration, held):
            first, last = iteration == 0, iteration == ITERS - 1
            before = () if first else (g.projected, g.state)
            g.projected, g.state, own = call(
                functools.partial(condense_kernel, first, held is not None),
                [((each, quarter), F32), state_of, message],
                *over_far(g.here), *before, *(() if held is None else (held,)), *inverse,
                flops=6 * quarter * quarter * each,
            )
            fresh = gathered_from(own)
            if not first:
                kept = () if iteration == 1 else (g.solution, g.gathered)
                g.direction, g.solution, g.gathered = call(
                    functools.partial(advance_kernel, iteration == 1), [field, field, ((4, each, quarter), F32)],
                    g.state, g.step, g.residual, g.direction, *g.coeffs, *kept,
                )
            g.coeffs = fresh
            if last:
                return own
            (spread,) = call(
                spread_kernel, [((2, each + EXTRA, half), F32)], *fresh, *back,
                scratch=[pltpu.VMEM((2 * each, width), BF16)], flops=work,
            )
            came = swap(spread[1], 1, 0)
            mine = over_leaf(spread[0] + came)
            other = swap(mine[:each], 1, 0)
            g.residual, g.step, messages = call(
                update_kernel, [field, ((each, LANES), F32), messages_of],
                g.state, mine, other, g.residual, g.direction, scale, high, low, flops=work,
            )
            g.here = over_near(messages)

        for iteration in range(ITERS):
            held = None
            for g in groups:
                held = iterate(g, iteration, held)
        energy = sum(one[each:, :LANES] for one in groups[-1].coeffs)
        energy = over_leaf(energy + swap(energy, 1, 0))
        ends = []
        for g in groups:
            ends += [g.state, g.direction, *g.coeffs, g.solution, g.gathered]
        solution, interior = call(
            finish_kernel, [((rows, columns), F32), ((blocks * rank, columns), F32)], interior, energy, *ends,
            scratch=[pltpu.VMEM((columns, blocks * rank), F32)],
        )
        return solution, interior.reshape(interior_load.shape)

    return per_device


def solution(mesh):
    return jax.shard_map(
        solver(mesh.shape["leaf"], mesh.shape["front"]),
        mesh=mesh,
        in_specs=(
            P(("wave", "front"), None),
            P("front"),
            P(("wave", "front")),
            P(("wave", "front"), "leaf"),
            P(("wave", "leaf"), None, None),
            P(("wave", "leaf"), None, None),
        ),
        out_specs=(P(("wave", "front"), None), P(("wave", "leaf"), None, None)),
        check_vma=False,
    )
```
